256 devices in a mesh: grp: 8 (over z), feat: 32 (over x, y, core).
Axes of the slice: x: 4, y: 4, z: 8, core: 2. Of those that a mesh axis runs over, the one named last changes fastest.
Arguments:
- features: bfloat16 [65536, 512], P(('grp', 'feat')), may hold values from -6 to 6
- adj_tiles: bfloat16 [512, 16, 128, 128], P(('grp', 'feat')), may hold values from 0.0099487305 to 1
- src_block: int32 [512, 16], P(('grp', 'feat')), may hold values from 0 to 63, as said below
- counts: int32 [512], P(('grp', 'feat')), may hold values from 1 to 16, as said below
- w_self: bfloat16 [512, 512], replicated, may hold values from -0.25 to 0.25
- w_neigh: bfloat16 [512, 512], replicated, may hold values from -0.25 to 0.25
- multiplier: float32 [512], replicated, may hold values from 0.5 to 2
- bit_shift: int32 [512], replicated, may hold values from 0 to 2
- cotangent: bfloat16 [65536, 512], P(('grp', 'feat')), may hold values from -6 to 6
Outputs:
- output: bfloat16 [65536, 512], P(('grp', 'feat'))
- grad_features: bfloat16 [65536, 512], P(('grp', 'feat'))
- grad_self: float32 [512, 512], replicated
- grad_neigh: float32 [512, 512], replicated
The draws below stay inside these ranges and needn't reach their ends.
Inputs may be any that keep to these rules, and one draw needn't show every extreme that they name: src_block[i, k] is a block of block i's own group, held by a device at most 2 positions from block i's device in the group's cyclic order of devices (block i is held by device (i % 64) // 2 of its group, which holds 2 consecutive blocks); the distance 2 is reached in both directions in every draw. Slots k >= counts[i] take no part.
All inputs are finite; a program needn't handle non-finite values.
Results may differ from the reference program's by a relative error of at most 0.0059.
Values may be sent and summed in bfloat16 or wider, within the bound.
No kernel may reach another device: no remote copies, remote signals or barrier semaphores. Data moves between devices by JAX's collectives and lax.ppermute only.
A program may use at most 64 MiB of HBM per device.

```python
import math
import jax
import jax.numpy as jnp
from jax import lax

F = 512
HID = 512
BLK = 128
B_DEV = 2
SLOTS = 16
SPAN = 2
BLOCKS_GRP = 64
BLOCKS = 512
NODES = 65536


def layout_draw(key):
    base = jax.random.fold_in(key, 11)
    key_a, key_b, key_c, key_d = jax.random.split(base, 4)
    spread_raw = jax.random.randint(key_a, (BLOCKS,), 0, SLOTS)
    slot_counts = 1 + spread_raw * spread_raw // SLOTS
    busiest = jax.random.randint(key_b, (), 0, BLOCKS)
    slot_counts = slot_counts.at[busiest].set(SLOTS)
    offsets = jax.random.randint(key_c, (BLOCKS, SLOTS), -SPAN, SPAN + 1)
    offsets = offsets.at[busiest, 0].set(SPAN).at[busiest, 1].set(-SPAN)
    local_pick = jax.random.randint(key_d, (BLOCKS, SLOTS), 0, B_DEV)
    group_width = BLOCKS_GRP // B_DEV
    home_dev = jnp.arange(BLOCKS, dtype=jnp.int32) % BLOCKS_GRP // B_DEV
    source_dev = (home_dev[:, None] + offsets) % group_width
    return (slot_counts.astype(jnp.int32), (source_dev * B_DEV + local_pick).astype(jnp.int32))


def draw_counts(key, part):
    return layout_draw(key)[0]


def draw_src_block(key, part):
    return layout_draw(key)[1]


def set_ends(entries, own_key, smallest, largest):
    longest = entries.shape.index(max(entries.shape))
    spots = []
    for shift in (0, 1):
        where = [jax.random.randint(jax.random.fold_in(own_key, axis), (), 0, length) for axis, length in enumerate(entries.shape)]
        where[longest] = (where[longest] + shift) % entries.shape[longest]
        spots.append(tuple(where))
    return entries.at[spots[0]].set(smallest).at[spots[1]].set(largest)


def levels(stream_key, dims, shards, low, top_value):
    gain, own = 1.0, jax.random.fold_in(stream_key, 6)
    for dim, shards_of in shards:
        heights = jnp.exp(jax.random.uniform(jax.random.fold_in(own, dim), (shards_of,), jnp.float32, low / len(shards), top_value / len(shards)))
        gain = gain * jnp.repeat(heights, dims[dim] // shards_of).reshape([-1 if axis == dim else 1 for axis in range(len(dims))])
    return gain


def scatter_about(own_key, dims, deviation, bound, cuts=(), held_as=jnp.bfloat16):
    factor_of = levels(own_key, dims, cuts, -0.22, 0.18) if cuts else 1.0
    array = jax.random.normal(own_key, dims, jnp.float32) * deviation * factor_of
    return jnp.minimum(jnp.maximum(array, -bound), bound).astype(held_as)


def setup_inputs(seed: int = 0) -> dict:
    arg_keys = jax.random.split(jax.random.key(seed), 10)
    return {
        "features": scatter_about(arg_keys[0], (NODES, F), 1.0, 6.0, ((0, 256),)),
        "adj_tiles": jnp.clip(jnp.exp(math.log(1.0) - 4.61031033 * jax.random.uniform(arg_keys[1], (BLOCKS, SLOTS, BLK, BLK), jnp.float32) ** levels(arg_keys[1], (BLOCKS, SLOTS, BLK, BLK), ((0, 256),), -0.2, 0.2)), 0.0099487305, 1.0).astype(jnp.bfloat16),
        "src_block": draw_src_block(jax.random.fold_in(arg_keys[9], 71), 0),
        "counts": draw_counts(jax.random.fold_in(arg_keys[9], 71), 0),
        "w_self": scatter_about(arg_keys[4], (F, HID), F ** -0.5, 0.25),
        "w_neigh": scatter_about(arg_keys[5], (F, HID), F ** -0.5, 0.25),
        "multiplier": jnp.clip(jnp.exp(jax.random.uniform(arg_keys[6], (HID,), jnp.float32, math.log(0.5), math.log(2.0))), 0.5, 2.0),
        "bit_shift": set_ends(jax.random.randint(arg_keys[7], (HID,), 0, 3), jax.random.fold_in(arg_keys[7], 1), 0, 2).astype(jnp.int32),
        "cotangent": scatter_about(arg_keys[8], (NODES, HID), 1.0, 6.0, ((0, 256),)),
    }


def reference(features, adj_tiles, src_block, counts, w_self, w_neigh, multiplier, bit_shift, cotangent):
    block_ids = jnp.arange(BLOCKS, dtype=jnp.int32)
    absolute = src_block + (block_ids // BLOCKS_GRP * BLOCKS_GRP)[:, None]
    live_mask = jnp.arange(SLOTS, dtype=jnp.int32)[None, :] < counts[:, None]
    masked = jnp.where(live_mask[:, :, None, None], adj_tiles, jnp.zeros_like(adj_tiles))
    degree = lax.optimization_barrier(jnp.sum(masked, axis=(1, 3), dtype=jnp.float32))
    inv_root = lax.rsqrt(degree)
    node_blocks = features.reshape(BLOCKS, BLK, F)

    def one_block(item):
        tile_set, where_src = item
        sources = node_blocks[where_src]
        return jnp.einsum('kij,kjf->if', tile_set.astype(jnp.float32), sources.astype(jnp.float32), precision=lax.Precision.HIGHEST)
    summed = lax.map(one_block, (masked, absolute))
    aggregated = (summed * inv_root[:, :, None]).astype(jnp.bfloat16).reshape(NODES, F)
    preact = jnp.dot(features, w_self, preferred_element_type=jnp.float32)
    preact = preact + jnp.dot(aggregated, w_neigh, preferred_element_type=jnp.float32)
    scale = multiplier * jnp.exp2(-bit_shift.astype(jnp.float32))
    scaled = preact * scale
    sigmoid_val = jax.nn.sigmoid(scaled)
    output = (scaled * sigmoid_val).astype(jnp.bfloat16)
    grad_pre = (cotangent.astype(jnp.float32) * sigmoid_val * (1.0 + scaled * (1.0 - sigmoid_val)) * scale).astype(jnp.bfloat16)
    grad_scale = 1.0 / math.sqrt(NODES)
    grad_self = jnp.dot(features.T, grad_pre, preferred_element_type=jnp.float32) * grad_scale
    grad_neigh = jnp.dot(aggregated.T, grad_pre, preferred_element_type=jnp.float32) * grad_scale
    own_part = jnp.dot(grad_pre, w_self.T, preferred_element_type=jnp.float32)
    back = jnp.dot(grad_pre, w_neigh.T, preferred_element_type=jnp.float32).reshape(BLOCKS, BLK, F)
    back = (back * inv_root[:, :, None]).astype(jnp.bfloat16)
    dev_count = BLOCKS // B_DEV
    tiles_dev = masked.reshape(dev_count, B_DEV, SLOTS, BLK, BLK)
    back_dev = back.reshape(dev_count, B_DEV, BLK, F)
    src_dev = src_block.reshape(dev_count, B_DEV * SLOTS)
    dev_ids = jnp.arange(dev_count, dtype=jnp.int32)

    def step(carry, item):
        dev_index, tile_set, back_rows, where_src = item
        contrib = jnp.einsum('bkij,bif->bkjf', tile_set.astype(jnp.float32), back_rows.astype(jnp.float32), precision=lax.Precision.HIGHEST).reshape(B_DEV * SLOTS, BLK, F)
        gathered = jax.ops.segment_sum(contrib, where_src, num_segments=BLOCKS_GRP)
        rounded = lax.optimization_barrier(gathered.astype(jnp.bfloat16)).astype(jnp.float32)
        base = (dev_index // (BLOCKS_GRP // B_DEV) * BLOCKS_GRP).astype(jnp.int32)
        current = lax.dynamic_slice_in_dim(carry, base, BLOCKS_GRP, 0)
        return (lax.dynamic_update_slice_in_dim(carry, current + rounded, base, 0), None)
    spread, _ = lax.scan(step, jnp.zeros((BLOCKS, BLK, F), jnp.float32), (dev_ids, tiles_dev, back_dev, src_dev))
    grad_features = (own_part + spread.reshape(NODES, F)).astype(jnp.bfloat16)
    return (output, grad_features, grad_self, grad_neigh)
```

```python
import math

import jax
import jax.numpy as jnp
from jax import lax
from jax.experimental import pallas as pl
from jax.experimental.pallas import tpu as pltpu
from jax.sharding import Mesh, PartitionSpec as P

SPAN = 2
WINDOW = 2 * SPAN + 1
BF16 = jnp.bfloat16
F32 = jnp.float32
AXES = ("z", "x", "y", "c")
FEAT = ("x", "y", "c")


def passed_along(x, by):
    peers = lax.axis_size(FEAT)
    return lax.ppermute(x, FEAT, [(i, (i + by) % peers) for i in range(peers)])


def to_partner(x):
    return lax.ppermute(x, "c", [(0, 1), (1, 0)])


def dot(a, b):
    return jnp.dot(a, b, preferred_element_type=F32)


def dot_tn(a, b):
    return lax.dot_general(a, b, (((0,), (0,)), ((), ())), preferred_element_type=F32)


def dot_nt(a, b):
    return lax.dot_general(a, b, (((1,), (1,)), ((), ())), preferred_element_type=F32)


def prepare_kernel(peers, where_ref, src_ref, counts_ref, adj_ref, a_ref, at_ref, inv_ref, acc_ref):
    num_blocks, num_slots, block_len, _ = adj_ref.shape
    window_count = acc_ref.shape[0]
    my_index = where_ref[0]
    acc_ref[...] = jnp.zeros(acc_ref.shape, F32)
    for block in range(num_blocks):
        rows = pl.ds(block * block_len, block_len)

        def add_slot(slot, carry, block=block, rows=rows):
            source = src_ref[block, slot]
            relative = lax.rem(source // num_blocks - my_index + SPAN + 2 * peers, peers)
            relative = jnp.minimum(relative, WINDOW - 1)
            place = relative * num_blocks + lax.rem(source, num_blocks)
            acc_ref[place, rows, :] += adj_ref[block, slot].astype(F32)
            return carry

        lax.fori_loop(0, jnp.minimum(counts_ref[block], num_slots), add_slot, 0)
    degree = jnp.zeros(acc_ref.shape[1:], F32)
    for place in range(window_count):
        strip = acc_ref[place]
        degree += strip
        columns = pl.ds(place * block_len, block_len)
        a_ref[:, columns] = strip.astype(BF16)
        at_ref[columns, :] = strip.T.astype(BF16)
    inv_root = lax.rsqrt(jnp.sum(degree, axis=1, keepdims=True))
    inv_ref[...] = jnp.broadcast_to(inv_root, inv_ref.shape)


def forward_kernel(
    core_ref, a_ref, own_ref, m2_ref, m1_ref, p1_ref, p2_ref, inv_ref, ws_ref, wn_ref, scale_ref, cot_ref,
    out_ref, grad_ref, keep_ref, send_ref,
):
    rows = own_ref.shape[0]
    own = own_ref[...]
    summed = jnp.zeros(own.shape, F32)
    for place, ref in enumerate((m2_ref, m1_ref, own_ref, p1_ref, p2_ref)):
        summed += dot(a_ref[:, pl.ds(place * rows, rows)], ref[...])
    aggregated = (summed * inv_ref[:, :1]).astype(BF16)
    preact = dot(own, ws_ref[...]) + dot(aggregated, wn_ref[...])
    scale = scale_ref[...]
    scaled = preact * scale
    sig = jax.nn.sigmoid(scaled)
    out_ref[...] = (scaled * sig).astype(BF16)
    grad = (cot_ref[...].astype(F32) * sig * (1.0 + scaled * (1.0 - sig)) * scale).astype(BF16)
    grad_ref[...] = grad
    first = core_ref[0] == 0
    keep_ref[...] = dot_tn(jnp.where(first, own, aggregated), grad)
    send_ref[...] = dot_tn(jnp.where(first, aggregated, own), grad).astype(BF16)


def backward_kernel(
    grad_ref, at_ref, inv_ref, ws_ref, wn_ref, base_ref, m2_ref, m1_ref, p1_ref, p2_ref
):
    grad = grad_ref[...]
    rows = grad.shape[0]
    back = (dot_nt(grad, wn_ref[...]) * inv_ref[:, :1]).astype(BF16)
    for place, ref in ((0, m2_ref), (1, m1_ref), (3, p1_ref), (4, p2_ref)):
        ref[...] = dot(at_ref[pl.ds(place * rows, rows), :], back).astype(BF16)
    own_term = dot(at_ref[pl.ds(SPAN * rows, rows), :], back).astype(BF16)
    base_ref[...] = dot_nt(grad, ws_ref[...]) + own_term.astype(F32)


def local(
    features, adj_tiles, src_block, counts, w_self, w_neigh, multiplier, bit_shift, cotangent
):
    num_blocks, _, block_len, _ = adj_tiles.shape
    row_count, width = features.shape
    hidden = w_self.shape[1]
    peers = lax.axis_size(FEAT)
    chips = lax.axis_size(("x", "y"))
    groups = lax.axis_size("z")
    my_index = lax.axis_index(FEAT).astype(jnp.int32).reshape(1)
    my_core = lax.axis_index("c").astype(jnp.int32).reshape(1)
    shape = jax.ShapeDtypeStruct
    vmem = pl.BlockSpec(memory_space=pltpu.VMEM)
    smem = pl.BlockSpec(memory_space=pltpu.SMEM)

    near = {by: passed_along(features, -by) for by in (-2, -1, 1, 2)}
    scale = (multiplier * jnp.exp2(-bit_shift.astype(F32))).reshape(1, hidden)
    columns = WINDOW * row_count
    adj, adj_t, inv_root = pl.pallas_call(
        lambda *refs: prepare_kernel(peers, *refs),
        out_shape=(
            shape((row_count, columns), BF16),
            shape((columns, row_count), BF16),
            shape((row_count, 128), F32),
        ),
        in_specs=[smem, smem, smem, vmem],
        out_specs=(vmem, vmem, vmem),
        scratch_shapes=[pltpu.VMEM((WINDOW * num_blocks, row_count, block_len), F32)],
        name="prepare",
    )(my_index, src_block, counts, adj_tiles)

    output, grad_pre, keep, send = pl.pallas_call(
        forward_kernel,
        out_shape=(
            shape((row_count, hidden), BF16),
            shape((row_count, hidden), BF16),
            shape((width, hidden), F32),
            shape((width, hidden), BF16),
        ),
        in_specs=[smem] + [vmem] * 11,
        out_specs=(vmem,) * 4,
        name="forward",
    )(
        my_core, adj, features, near[-2], near[-1], near[1], near[2], inv_root, w_self, w_neigh, scale, cotangent,
    )
    received = to_partner(send)

    base, *terms = pl.pallas_call(
        backward_kernel,
        out_shape=(shape((row_count, width), F32),) + (shape((row_count, width), BF16),) * 4,
        in_specs=[vmem] * 5,
        out_specs=(vmem,) * 5,
        name="backward",
    )(grad_pre, adj_t, inv_root, w_self, w_neigh)
    arrived = [passed_along(term, by) for term, by in zip(terms, (-2, -1, 1, 2))]

    piece_rows = width // chips
    pair = (keep + received.astype(F32)).astype(BF16).reshape(chips, piece_rows, hidden)
    pieces = lax.all_to_all(pair, ("x", "y"), 0, 0)
    plane = jnp.sum(pieces.astype(F32), axis=0).astype(BF16)
    planes = lax.all_to_all(jnp.broadcast_to(plane, (groups,) + plane.shape), "z", 0, 0)
    grad_scale = 1.0 / math.sqrt(row_count * groups * peers)
    total = (jnp.sum(planes.astype(F32), axis=0) * grad_scale).astype(BF16)
    mine = lax.all_to_all(jnp.broadcast_to(total, (chips,) + total.shape), ("x", "y"), 0, 0)
    mine = mine.reshape(width, hidden)
    other = to_partner(mine)
    first = my_core[0] == 0
    grad_self = jnp.where(first, mine, other).astype(F32)
    grad_neigh = jnp.where(first, other, mine).astype(F32)

    spread = base
    for term in arrived:
        spread = spread + term.astype(F32)
    return output, spread.astype(BF16), grad_self, grad_neigh


def solution(mesh):
    feat = mesh.shape["feat"]
    fine = Mesh(mesh.devices.reshape(mesh.shape["grp"], 4, feat // 8, 2), AXES)
    nodes = P(AXES)
    return jax.shard_map(
        local,
        mesh=fine,
        in_specs=(nodes, nodes, nodes, nodes, P(), P(), P(), P(), nodes),
        out_specs=(nodes, nodes, P(), P()),
        check_vma=False,
    )
```

```python
import math

import jax
import jax.numpy as jnp
from jax import lax
from jax.experimental import pallas as pl
from jax.experimental.pallas import tpu as pltpu
from jax.sharding import Mesh, PartitionSpec as P


SPAN = 2
WINDOW = 2 * SPAN + 1
BF16 = jnp.bfloat16
F32 = jnp.float32
AXES = ("z", "x", "y", "c")
FEAT = ("x", "y", "c")


def passed_along(x, by):
    peers = lax.axis_size(FEAT)
    return lax.ppermute(x, FEAT, [(i, (i + by) % peers) for i in range(peers)])


def to_partner(x):
    return lax.ppermute(x, "c", [(0, 1), (1, 0)])


def dot(a, b):
    return jnp.dot(a, b, preferred_element_type=F32)


def dot_tn(a, b):
    return lax.dot_general(a, b, (((0,), (0,)), ((), ())), preferred_element_type=F32)


def dot_nt(a, b):
    return lax.dot_general(a, b, (((1,), (1,)), ((), ())), preferred_element_type=F32)


def near(shape, dtype):
    return pltpu.VMEM(shape, dtype)


def far(shape, dtype):
    return pltpu.HBM(shape, dtype)


def call(kernel, scalars, arrays, outs, scratch=()):
    smem = pl.BlockSpec(memory_space=pltpu.SMEM)
    vmem = pl.BlockSpec(memory_space=pltpu.VMEM)
    held = [pltpu.with_memory_space_constraint(a, pltpu.VMEM) for a in arrays]
    return pl.pallas_call(
        kernel,
        out_shape=tuple(outs),
        in_specs=[smem] * len(scalars) + [vmem] * len(held),
        out_specs=(vmem,) * len(outs),
        scratch_shapes=scratch,
        compiler_params=pltpu.CompilerParams(vmem_limit_bytes=16 * 1024 * 1024),
    )(*scalars, *held)


def prepare_kernel(peers, where_ref, src_ref, counts_ref, adj_ref, a_ref, at_ref, inv_ref, acc_ref):
    num_blocks, num_slots, block_len, _ = adj_ref.shape
    window_count = acc_ref.shape[0]
    my_index = where_ref[0]
    acc_ref[...] = jnp.zeros(acc_ref.shape, F32)
    for block in range(num_blocks):
        rows = pl.ds(block * block_len, block_len)

        def add_slot(slot, carry, block=block, rows=rows):
            source = src_ref[block, slot]
            relative = lax.rem(source // num_blocks - my_index + SPAN + 2 * peers, peers)
            relative = jnp.minimum(relative, WINDOW - 1)
            place = relative * num_blocks + lax.rem(source, num_blocks)
            acc_ref[place, rows, :] += adj_ref[block, slot].astype(F32)
            return carry

        lax.fori_loop(0, jnp.minimum(counts_ref[block], num_slots), add_slot, 0)
    degree = jnp.zeros(acc_ref.shape[1:], F32)
    for place in range(window_count):
        strip = acc_ref[place]
        degree += strip
        columns = pl.ds(place * block_len, block_len)
        a_ref[:, columns] = strip.astype(BF16)
        at_ref[columns, :] = strip.T.astype(BF16)
    inv_root = lax.rsqrt(jnp.sum(degree, axis=1, keepdims=True))
    inv_ref[...] = jnp.broadcast_to(inv_root, inv_ref.shape)


def forward_kernel(
    core_ref, a_ref, own_ref, m2_ref, m1_ref, p1_ref, p2_ref, inv_ref, ws_ref, wn_ref, scale_ref, cot_ref,
    out_ref, grad_ref, keep_ref, send_ref,
):
    rows = own_ref.shape[0]
    own = own_ref[...]
    summed = jnp.zeros(own.shape, F32)
    for place, ref in enumerate((m2_ref, m1_ref, own_ref, p1_ref, p2_ref)):
        summed += dot(a_ref[:, pl.ds(place * rows, rows)], ref[...])
    aggregated = (summed * inv_ref[:, :1]).astype(BF16)
    preact = dot(own, ws_ref[...]) + dot(aggregated, wn_ref[...])
    scale = scale_ref[...]
    scaled = preact * scale
    sig = jax.nn.sigmoid(scaled)
    out_ref[...] = (scaled * sig).astype(BF16)
    grad = (cot_ref[...].astype(F32) * sig * (1.0 + scaled * (1.0 - sig)) * scale).astype(BF16)
    grad_ref[...] = grad
    first = core_ref[0] == 0
    keep_ref[...] = dot_tn(jnp.where(first, own, aggregated), grad)
    send_ref[...] = dot_tn(jnp.where(first, aggregated, own), grad).astype(BF16)


def backward_kernel(
    grad_ref, at_ref, inv_ref, ws_ref, wn_ref, base_ref, m2_ref, m1_ref, p1_ref, p2_ref
):
    grad = grad_ref[...]
    rows = grad.shape[0]
    back = (dot_nt(grad, wn_ref[...]) * inv_ref[:, :1]).astype(BF16)
    for place, ref in ((0, m2_ref), (1, m1_ref), (3, p1_ref), (4, p2_ref)):
        ref[...] = dot(at_ref[pl.ds(place * rows, rows), :], back).astype(BF16)
    own_term = dot(at_ref[pl.ds(SPAN * rows, rows), :], back).astype(BF16)
    base_ref[...] = dot_nt(grad, ws_ref[...]) + own_term.astype(F32)


def pair_kernel(keep_ref, received_ref, pair_ref):
    pair = keep_ref[...] + received_ref[...].astype(F32)
    pair_ref[...] = pair.astype(BF16).reshape(pair_ref.shape)


def sum_kernel(factor, pieces_ref, copies_ref):
    total = pieces_ref[0].astype(F32)
    for piece in range(1, pieces_ref.shape[0]):
        total += pieces_ref[piece].astype(F32)
    total = (total * factor).astype(BF16)
    for copy in range(copies_ref.shape[0]):
        copies_ref[copy] = total


def spread_kernel(base_ref, *refs):
    *terms, out_ref = refs
    spread = base_ref[...]
    for term in terms:
        spread += term[...].astype(F32)
    out_ref[...] = spread.astype(BF16)


def weights_kernel(core_ref, mine_ref, other_ref, self_ref, neigh_ref):
    first = core_ref[0] == 0
    mine = mine_ref[...].reshape(self_ref.shape)
    other = other_ref[...].reshape(self_ref.shape)
    self_ref[...] = jnp.where(first, mine, other).astype(F32)
    neigh_ref[...] = jnp.where(first, other, mine).astype(F32)


def local(
    features, adj_tiles, src_block, counts, w_self, w_neigh, multiplier, bit_shift, cotangent
):
    num_blocks, _, block_len, _ = adj_tiles.shape
    row_count, width = features.shape
    hidden = w_self.shape[1]
    peers = lax.axis_size(FEAT)
    chips = lax.axis_size(("x", "y"))
    groups = lax.axis_size("z")
    my_index = lax.axis_index(FEAT).astype(jnp.int32).reshape(1)
    my_core = lax.axis_index("c").astype(jnp.int32).reshape(1)

    pulled = [passed_along(features, -by) for by in (-2, -1, 1, 2)]
    scale = (multiplier * jnp.exp2(-bit_shift.astype(F32))).reshape(1, hidden)
    columns = WINDOW * row_count
    adj, adj_t, inv_root = call(
        lambda *refs: prepare_kernel(peers, *refs),
        (my_index, src_block, counts),
        (adj_tiles,),
        (near((row_count, columns), BF16), near((columns, row_count), BF16), near((row_count, 128), F32)),
        [pltpu.VMEM((WINDOW * num_blocks, row_count, block_len), F32)],
    )
    output, grad_pre, keep, send = call(
        forward_kernel,
        (my_core,),
        (adj, features, *pulled, inv_root, w_self, w_neigh, scale, cotangent),
        (
            far((row_count, hidden), BF16),
            near((row_count, hidden), BF16),
            near((width, hidden), F32),
            near((width, hidden), BF16),
        ),
    )
    received = to_partner(send)
    piece_rows = width // chips
    (pair,) = call(pair_kernel, (), (keep, received), (far((chips, piece_rows, hidden), BF16),))
    base, *terms = call(
        backward_kernel,
        (),
        (grad_pre, adj_t, inv_root, w_self, w_neigh),
        (far((row_count, width), F32),) + (far((row_count, width), BF16),) * 4,
    )

    pieces = lax.all_to_all(pair, ("x", "y"), 0, 0)
    (plane,) = call(lambda *refs: sum_kernel(1.0, *refs), (), (pieces,), (far((groups, piece_rows, hidden), BF16),))
    arrived = [passed_along(term, by) for term, by in zip(terms, (-2, -1, 1, 2))]
    planes = lax.all_to_all(plane, "z", 0, 0)
    grad_scale = 1.0 / math.sqrt(row_count * groups * peers)
    (total,) = call(
        lambda *refs: sum_kernel(grad_scale, *refs), (), (planes,), (far((chips, piece_rows, hidden), BF16),)
    )
    mine = lax.all_to_all(total, ("x", "y"), 0, 0)
    (grad_features,) = call(spread_kernel, (), (base, *arrived), (far((row_count, width), BF16),))
    other = to_partner(mine)
    grad_self, grad_neigh = call(weights_kernel, (my_core,), (mine, other), (far((width, hidden), F32),) * 2)
    return output, grad_features, grad_self, grad_neigh


def solution(mesh):
    feat = mesh.shape["feat"]
    fine = Mesh(mesh.devices.reshape(mesh.shape["grp"], 4, feat // 8, 2), AXES)
    nodes = P(AXES)

    return jax.shard_map(
        local,
        mesh=fine,
        in_specs=(nodes, nodes, nodes, nodes, P(), P(), P(), P(), nodes),
        out_specs=(nodes, nodes, P(), P()),
        check_vma=False,
    )
```

```python
import math

import jax
import jax.numpy as jnp
from jax import lax
from jax.experimental import pallas as pl
from jax.experimental.pallas import tpu as pltpu
from jax.sharding import Mesh, PartitionSpec as P


SPAN = 2
WINDOW = 2 * SPAN + 1
BF16 = jnp.bfloat16
F32 = jnp.float32
AXES = ("z", "x", "y", "c")
FEAT = ("x", "y", "c")


def passed_along(x, by):
    peers = lax.axis_size(FEAT)
    return lax.ppermute(x, FEAT, [(i, (i + by) % peers) for i in range(peers)])


def to_partner(x):
    return lax.ppermute(x, "c", [(0, 1), (1, 0)])


def dot(a, b):
    return jnp.dot(a, b, preferred_element_type=F32)


def dot_tn(a, b):
    return lax.dot_general(a, b, (((0,), (0,)), ((), ())), preferred_element_type=F32)


def dot_nt(a, b):
    return lax.dot_general(a, b, (((1,), (1,)), ((), ())), preferred_element_type=F32)


def near(shape, dtype):
    return pltpu.VMEM(shape, dtype)


def far(shape, dtype):
    return pltpu.HBM(shape, dtype)


def call(kernel, scalars, arrays, outs, scratch=(), remote=(), written=False, aliases=None):
    smem = pl.BlockSpec(memory_space=pltpu.SMEM)
    vmem = pl.BlockSpec(memory_space=pltpu.VMEM)
    hbm = pl.BlockSpec(memory_space=pltpu.HBM)
    held = [pltpu.with_memory_space_constraint(a, pltpu.VMEM) for a in arrays]
    return pl.pallas_call(
        kernel,
        out_shape=tuple(outs),
        in_specs=[smem] * len(scalars) + [vmem] * len(held) + [hbm] * len(remote),
        out_specs=(hbm if written else vmem,) * len(outs),
        input_output_aliases=aliases or {},
        scratch_shapes=scratch,
        compiler_params=pltpu.CompilerParams(vmem_limit_bytes=16 * 1024 * 1024),
    )(*scalars, *held, *remote)


def prepare_kernel(
    peers, where_ref, src_ref, counts_ref, adj_ref, mult_ref, shift_ref, feat_ref, cot_ref,
    a_ref, at_ref, inv_ref, own_ref, held_ref, scale_ref, acc_ref, sems,
):
    num_blocks, num_slots, block_len, _ = adj_ref.shape
    window_count = acc_ref.shape[0]
    my_index = where_ref[0]
    pulls = [
        pltpu.make_async_copy(feat_ref, own_ref, sems.at[0]),
        pltpu.make_async_copy(cot_ref, held_ref, sems.at[1]),
    ]
    for pull in pulls:
        pull.start()
    scale_ref[...] = mult_ref[...] / jnp.left_shift(1, shift_ref[...]).astype(F32)
    acc_ref[...] = jnp.zeros(acc_ref.shape, F32)
    for block in range(num_blocks):
        rows = pl.ds(block * block_len, block_len)

        def add_slot(slot, carry, block=block, rows=rows):
            source = src_ref[block, slot]
            relative = lax.rem(source // num_blocks - my_index + SPAN + 2 * peers, peers)
            relative = jnp.minimum(relative, WINDOW - 1)
            place = relative * num_blocks + lax.rem(source, num_blocks)
            acc_ref[place, rows, :] += adj_ref[block, slot].astype(F32)
            return carry

        lax.fori_loop(0, jnp.minimum(counts_ref[block], num_slots), add_slot, 0)
    degree = jnp.zeros(acc_ref.shape[1:], F32)
    for place in range(window_count):
        strip = acc_ref[place]
        degree += strip
        columns = pl.ds(place * block_len, block_len)
        a_ref[:, columns] = strip.astype(BF16)
        at_ref[columns, :] = strip.T.astype(BF16)
    inv_root = lax.rsqrt(jnp.sum(degree, axis=1, keepdims=True))
    inv_ref[...] = jnp.broadcast_to(inv_root, inv_ref.shape)
    for pull in pulls:
        pull.wait()


def forward_kernel(
    core_ref, a_ref, own_ref, m2_ref, p2_ref, partner_ref, m1_ref, p1_ref, inv_ref, ws_ref, wn_ref, scale_ref,
    cot_ref, out_ref, mine_ref,
):
    rows = own_ref.shape[0]
    first = core_ref[0] == 0
    own = own_ref[...]
    partner = partner_ref[...]
    blocks = (
        m2_ref[...],
        jnp.where(first, m1_ref[...], partner),
        own,
        jnp.where(first, partner, p1_ref[...]),
        p2_ref[...],
    )
    summed = jnp.zeros(own.shape, F32)
    for place, block in enumerate(blocks):
        summed += dot(a_ref[:, pl.ds(place * rows, rows)], block)
    aggregated = (summed * inv_ref[:, :1]).astype(BF16)
    mine_ref[1] = aggregated
    preact = dot(own, ws_ref[...]) + dot(aggregated, wn_ref[...])
    scale = scale_ref[...]
    scaled = preact * scale
    sig = jax.nn.sigmoid(scaled)
    out_ref[...] = (scaled * sig).astype(BF16)
    grad = cot_ref[...].astype(F32) * sig * (1.0 + scaled * (1.0 - sig)) * scale
    mine_ref[0] = grad.astype(BF16)


def backward_kernel(
    mine_ref, at_ref, inv_ref, ws_ref, wn_ref, base_ref, m2_ref, m1_ref, p1_ref, p2_ref
):
    grad = mine_ref[0]
    rows = grad.shape[0]
    back = (dot_nt(grad, wn_ref[...]) * inv_ref[:, :1]).astype(BF16)
    for place, ref in ((0, m2_ref), (1, m1_ref), (3, p1_ref), (4, p2_ref)):
        ref[...] = dot(at_ref[pl.ds(place * rows, rows), :], back).astype(BF16)
    own_term = dot(at_ref[pl.ds(SPAN * rows, rows), :], back).astype(BF16)
    base_ref[...] = dot_nt(grad, ws_ref[...]) + own_term.astype(F32)


def pair_kernel(core_ref, own_ref, partner_ref, mine_ref, theirs_ref, pair_ref):
    first = core_ref[0] == 0
    pair = dot_tn(jnp.where(first, own_ref[...], mine_ref[1]), mine_ref[0])
    pair += dot_tn(jnp.where(first, partner_ref[...], theirs_ref[1]), theirs_ref[0])
    pair_ref[...] = pair.astype(BF16).reshape(pair_ref.shape)


def sum_kernel(factor, pieces_ref, copies_ref):
    total = pieces_ref[0].astype(F32)
    for piece in range(1, pieces_ref.shape[0]):
        total += pieces_ref[piece].astype(F32)
    total = (total * factor).astype(BF16)
    for copy in range(copies_ref.shape[0]):
        copies_ref[copy] = total


def spread_kernel(base_ref, *refs):
    *terms, out_ref = refs
    spread = base_ref[...]
    for term in terms:
        spread += term[...].astype(F32)
    out_ref[...] = spread.astype(BF16)


def widen(to_self, matrix_ref, self_ref, neigh_ref, wide_ref, sems):
    parts = sems.shape[0]
    pieces = matrix_ref.shape[0] // parts
    rows = wide_ref.shape[0] // parts
    for part in range(parts):
        here = pl.ds(part * rows, rows)
        matrix = matrix_ref[pl.ds(part * pieces, pieces)]
        wide_ref[here, :] = matrix.reshape(rows, wide_ref.shape[1]).astype(F32)

        @pl.when(to_self)
        def _(part=part, here=here):
            pltpu.make_async_copy(wide_ref.at[here], self_ref.at[here], sems.at[part]).start()

        @pl.when(jnp.logical_not(to_self))
        def _(part=part, here=here):
            pltpu.make_async_copy(wide_ref.at[here], neigh_ref.at[here], sems.at[part]).start()

    for part in range(parts):
        here = pl.ds(part * rows, rows)
        pltpu.make_async_copy(wide_ref.at[here], self_ref.at[here], sems.at[part]).wait()


def write_mine_kernel(core_ref, matrix_ref, self_ref, neigh_ref, wide_ref, sems):
    widen(core_ref[0] == 0, matrix_ref, self_ref, neigh_ref, wide_ref, sems)


def write_other_kernel(core_ref, matrix_ref, self_in, neigh_in, self_ref, neigh_ref, wide_ref, sems):
    widen(core_ref[0] != 0, matrix_ref, self_ref, neigh_ref, wide_ref, sems)


def local(
    features, adj_tiles, src_block, counts, w_self, w_neigh, multiplier, bit_shift, cotangent
):
    num_blocks, _, block_len, _ = adj_tiles.shape
    row_count, width = features.shape
    hidden = w_self.shape[1]
    peers = lax.axis_size(FEAT)
    chips = lax.axis_size(("x", "y"))
    groups = lax.axis_size("z")
    my_index = lax.axis_index(FEAT).astype(jnp.int32).reshape(1)
    my_core = lax.axis_index("c").astype(jnp.int32).reshape(1)

    m2 = passed_along(features, 2)
    p2 = passed_along(features, -2)
    partner = to_partner(features)
    m1 = to_partner(m2)
    p1 = to_partner(p2)
    columns = WINDOW * row_count
    rows = (row_count, width)
    adj, adj_t, inv_root, own, held, scale = call(
        lambda *refs: prepare_kernel(peers, *refs),
        (my_index, src_block, counts),
        (adj_tiles, multiplier.reshape(1, -1), bit_shift.reshape(1, -1)),
        (
            near((row_count, columns), BF16),
            near((columns, row_count), BF16),
            near((row_count, 128), F32),
            near(rows, BF16),
            near((row_count, hidden), BF16),
            near((1, hidden), F32),
        ),
        [pltpu.VMEM((WINDOW * num_blocks, row_count, block_len), F32), pltpu.SemaphoreType.DMA((2,))],
        remote=(features, cotangent),
    )
    output, mine = call(
        forward_kernel,
        (my_core,),
        (adj, own, m2, p2, partner, m1, p1, inv_root, w_self, w_neigh, scale, held),
        (far((row_count, hidden), BF16), near((2, row_count, hidden), BF16)),
    )
    theirs = to_partner(mine)
    piece_rows = width // chips
    (pair,) = call(pair_kernel, (my_core,), (own, partner, mine, theirs), (far((chips, piece_rows, hidden), BF16),))
    base, *terms = call(
        backward_kernel,
        (),
        (mine, adj_t, inv_root, w_self, w_neigh),
        (far((row_count, width), F32),) + (far((row_count, width), BF16),) * 4,
    )

    pieces = lax.all_to_all(pair, ("x", "y"), 0, 0)
    (plane,) = call(lambda *refs: sum_kernel(1.0, *refs), (), (pieces,), (far((groups, piece_rows, hidden), BF16),))
    arrived = [passed_along(term, by) for term, by in zip(terms, (-2, -1, 1, 2))]
    planes = lax.all_to_all(plane, "z", 0, 0)
    grad_scale = 1.0 / math.sqrt(row_count * groups * peers)
    (total,) = call(
        lambda *refs: sum_kernel(grad_scale, *refs), (), (planes,), (far((chips, piece_rows, hidden), BF16),)
    )
    matrix = lax.all_to_all(total, ("x", "y"), 0, 0)
    (grad_features,) = call(spread_kernel, (), (base, *arrived), (far((row_count, width), BF16),))
    other = to_partner(matrix)
    outs = (far((width, hidden), F32),) * 2
    scratch = [pltpu.VMEM((width, hidden), F32), pltpu.SemaphoreType.DMA((4,))]
    written = call(write_mine_kernel, (my_core,), (matrix,), outs, scratch, written=True)
    grad_self, grad_neigh = call(
        write_other_kernel, (my_core,), (other,), outs, scratch, remote=written, written=True, aliases={2: 0, 3: 1}
    )
    return output, grad_features, grad_self, grad_neigh


def solution(mesh):
    feat = mesh.shape["feat"]
    fine = Mesh(mesh.devices.reshape(mesh.shape["grp"], 4, feat // 8, 2), AXES)
    nodes = P(AXES)

    return jax.shard_map(
        local,
        mesh=fine,
        in_specs=(nodes, nodes, nodes, nodes, P(), P(), P(), P(), nodes),
        out_specs=(nodes, nodes, P(), P()),
        check_vma=False,
    )
```
